32 devices in a mesh: gx: 4 (over z), gy: 2 (over y), gz: 4 (over x, core).
Axes of the slice: x: 2, y: 2, z: 4, core: 2. Of those that a mesh axis runs over, the one named last changes fastest.
Arguments:
- positions: float32 [8, 4, 8, 3, 128], P('gx', 'gy', 'gz'), may hold values from 0 to 64, as said below
- velocities: float32 [8, 4, 8, 3, 128], P('gx', 'gy', 'gz'), may hold values from -5 to 5
- species: int32 [8, 4, 8, 128], P('gx', 'gy', 'gz'), may hold values from 0 to 3, as said below
- neighbour_blocks: int32 [8, 4, 8, 8], P('gx', 'gy', 'gz'), may hold values from 0 to 27, as said below
- embedding: bfloat16 [4, 64], replicated, may hold values from -6 to 6
- w_send: bfloat16 [2, 64, 64], replicated, may hold values from -0.75 to 0.75
- w_radial: float32 [2, 8, 64], replicated, may hold values from -4 to 4
- w_update: bfloat16 [2, 64, 64], replicated, may hold values from -0.75 to 0.75
- w_out: bfloat16 [64, 64], replicated, may hold values from -0.75 to 0.75
- w_energy: float32 [64], replicated, may hold values from -5 to 5
- masses: float32 [4], replicated, may hold values from 0.5 to 8
Outputs:
- displacement: float32 [8, 4, 8, 3, 128], P('gx', 'gy', 'gz')
- new_velocity: float32 [8, 4, 8, 3, 128], P('gx', 'gy', 'gz')
The draws below stay inside these ranges and needn't reach their ends.
Inputs may be any that keep to these rules, and one draw needn't show every extreme that they name: `positions`: each atom slot lies in the cube of side 8 whose lowest corner is 8 times its block's coordinates. `species`: 0 marks an empty slot; in each block the empty slots follow the occupied ones, and at least 32 slots are occupied. `neighbour_blocks`: entry o below 27 is the offset 9 (dx + 1) + 3 (dy + 1) + (dz + 1) of a source block; 27 marks an empty slot. The first entry is 13, the block itself; live entries of a block are distinct and come before its empty slots; each block has two or more live entries.
All inputs are finite; a program needn't handle non-finite values.
Results may differ from the reference program's by a relative error of at most 0.039.
Values may be sent and summed in bfloat16 or wider, within the bound.
A program may use at most 64 MiB of HBM per device.

```python
import math
import jax
import jax.numpy as jnp
from jax import lax

C = 64
K = 8
SPECIES = 4
A = 128
NT = 8
STEPS = 1
NBX = 8
NBY = 4
NBZ = 8


block_side = 8.0


def draw_positions(key, part):
    full_shape = (NBX, NBY, NBZ, 3, A)
    component = lax.broadcasted_iota(jnp.int32, full_shape, 3)
    index_x = lax.broadcasted_iota(jnp.float32, full_shape, 0)
    index_y = lax.broadcasted_iota(jnp.float32, full_shape, 1)
    index_z = lax.broadcasted_iota(jnp.float32, full_shape, 2)
    anchor = jnp.where(component == 0, index_x, jnp.where(component == 1, index_y, index_z)) * block_side
    unit_draw = jax.random.uniform(jax.random.fold_in(key, 11), full_shape, jnp.float32)
    return anchor + block_side * unit_draw


def draw_velocities(key, part):
    full_shape = (NBX, NBY, NBZ, 3, A)
    frac_x = lax.broadcasted_iota(jnp.float32, full_shape, 0) / (NBX - 1)
    frac_y = lax.broadcasted_iota(jnp.float32, full_shape, 1) / (NBY - 1)
    frac_z = lax.broadcasted_iota(jnp.float32, full_shape, 2) / (NBZ - 1)
    spread = 0.15 * jnp.exp(0.5 * jnp.log(3.0) * (frac_x + frac_y + frac_z))
    base = jnp.clip(jax.random.normal(jax.random.fold_in(key, 42), full_shape, jnp.float32), -6.0, 6.0)
    return base * spread


def draw_species(key, part):
    key_fill = jax.random.fold_in(key, 21)
    key_kind = jax.random.fold_in(key, 22)
    filled = jax.random.randint(key_fill, (NBX, NBY, NBZ, 1), A // 4, A + 1)
    species_draw = jax.random.randint(key_kind, (NBX, NBY, NBZ, A), 1, SPECIES)
    slot_index = lax.broadcasted_iota(jnp.int32, (NBX, NBY, NBZ, A), 3)
    return jnp.where(slot_index < filled, species_draw, 0).astype(jnp.int32)


def draw_neighbour_blocks(key, part):
    key_rank = jax.random.fold_in(key, 31)
    key_count = jax.random.fold_in(key, 32)
    scores = jax.random.randint(key_rank, (NBX, NBY, NBZ, 26), 0, 1 << 20) * 32
    scores = scores + lax.broadcasted_iota(jnp.int32, (NBX, NBY, NBZ, 26), 3)
    ranking = jnp.argsort(scores, axis=-1, stable=True).astype(jnp.int32)
    others = ranking + (ranking >= 13).astype(jnp.int32)
    listing = jnp.concatenate([jnp.full((NBX, NBY, NBZ, 1), 13, jnp.int32), others[..., :NT - 1]], axis=-1)
    live_count = jax.random.randint(key_count, (NBX, NBY, NBZ, 1), 2, NT + 1)
    slot_index = lax.broadcasted_iota(jnp.int32, (NBX, NBY, NBZ, NT), 3)
    return jnp.where(slot_index < live_count, listing, 27).astype(jnp.int32)


def bell_draw(stream_key, extent, width, reach, kind=jnp.bfloat16):
    return jnp.clip(width * jax.random.normal(stream_key, extent, jnp.float32), -reach, reach).astype(kind)


def setup_inputs(seed: int = 0) -> dict:
    splits = jax.random.split(jax.random.key(seed), 12)
    positions = draw_positions(jax.random.fold_in(splits[11], 71), 0)
    velocities = draw_velocities(jax.random.fold_in(splits[11], 71), 0)
    species = draw_species(jax.random.fold_in(splits[11], 71), 0)
    neighbour_blocks = draw_neighbour_blocks(jax.random.fold_in(splits[11], 71), 0)
    embedding = bell_draw(splits[4], (SPECIES, C), 1.0, 6.0)
    w_send = bell_draw(splits[5], (2, C, C), C ** -0.5, 0.75)
    w_radial = bell_draw(splits[6], (2, K, C), 0.3, 4.0, jnp.float32)
    w_update = bell_draw(splits[7], (2, C, C), C ** -0.5, 0.75)
    w_out = bell_draw(splits[8], (C, C), C ** -0.5, 0.75)
    w_energy = bell_draw(splits[9], (C,), 0.35, 5.0, jnp.float32)
    masses = jnp.clip(jnp.exp(jax.random.uniform(splits[10], (SPECIES,), jnp.float32, math.log(0.5), math.log(8.0))), 0.5, 8.0)
    return {"positions": positions, "velocities": velocities, "species": species, "neighbour_blocks": neighbour_blocks, "embedding": embedding, "w_send": w_send, "w_radial": w_radial, "w_update": w_update, "w_out": w_out, "w_energy": w_energy, "masses": masses}


soft_sq = 0.25
cut_sq = 25.0
gamma_width = 2.56
time_step = 1.0
target_slot = 0.25
tiny_eps = 1e-06

def slot_tables(neighbour_blocks):
    size_x, size_y, size_z, slot_count = neighbour_blocks.shape
    is_live = neighbour_blocks < 27
    offset = jnp.where(is_live, neighbour_blocks, 13)
    step_x = offset // 9 - 1
    step_y = offset // 3 % 3 - 1
    step_z = offset % 3 - 1
    index_x = lax.broadcasted_iota(jnp.int32, neighbour_blocks.shape, 0)
    index_y = lax.broadcasted_iota(jnp.int32, neighbour_blocks.shape, 1)
    index_z = lax.broadcasted_iota(jnp.int32, neighbour_blocks.shape, 2)
    source = ((index_x + 1 + step_x) * (size_y + 2) + (index_y + 1 + step_y)) * (size_z + 2) + (index_z + 1 + step_z)
    target = ((index_x[..., 0] + 1) * (size_y + 2) + index_y[..., 0] + 1) * (size_z + 2) + index_z[..., 0] + 1
    return (source.reshape(-1, slot_count).astype(jnp.int32), target.reshape(-1).astype(jnp.int32), is_live.astype(jnp.float32).reshape(-1, slot_count), (neighbour_blocks == 13).astype(jnp.float32).reshape(-1, slot_count))

def feature_table(species_ext, embedding):
    kind_count = embedding.shape[0]
    onehot = (species_ext[..., None, :] == lax.broadcasted_iota(jnp.int32, (kind_count, 1), 0)).astype(jnp.float32)
    return jnp.einsum('sc,...sa->...ca', embedding.astype(jnp.float32), onehot)

def inverse_mass(species, masses):
    kind_count = masses.shape[0]
    onehot = (species[..., None, :] == lax.broadcasted_iota(jnp.int32, (kind_count, 1), 0)).astype(jnp.float32)
    return 1.0 / jnp.einsum('s,...sa->...a', masses, onehot)[..., None, :]

def pair_kernel(target_pos, target_real, source_pos, source_real, slot_live, slot_self, basis_count):
    offset = source_pos[:, :, None, :] - target_pos[None, :, :, None]
    squared = lax.optimization_barrier(jnp.sum(offset * offset, axis=1))
    distance = jnp.sqrt(squared + soft_sq)
    cutoff = jnp.square(jax.nn.relu(1.0 - squared / cut_sq))
    atom_count = target_pos.shape[-1]
    diagonal = (lax.broadcasted_iota(jnp.int32, (atom_count, atom_count), 0) == lax.broadcasted_iota(jnp.int32, (atom_count, atom_count), 1)).astype(jnp.float32)
    weight = cutoff * target_real[None, :, None] * source_real[:, None, :] * slot_live[:, None, None]
    weight = weight * (1.0 - slot_self[:, None, None] * diagonal[None])
    centers = (lax.iota(jnp.float32, basis_count) + 0.5) * (5.0 / basis_count)
    radial = jnp.exp(-gamma_width * jnp.square(distance[None] - centers[:, None, None, None]))
    return (weight[None] * radial).astype(jnp.bfloat16)

def block_message(kernel, source_feat, w_send, w_radial):
    sender = jnp.einsum('qcj,cd->qdj', source_feat.astype(jnp.bfloat16).astype(jnp.float32), w_send.astype(jnp.float32)).astype(jnp.bfloat16)
    partial_value = jnp.einsum('kqij,qdj->kdi', kernel.astype(jnp.float32), sender.astype(jnp.float32))
    return lax.optimization_barrier(jnp.sum(partial_value * w_radial[:, :, None], axis=0)).astype(jnp.bfloat16)

def block_update(target_feat, message, w_update):
    update = jnp.einsum('ci,cd->di', message.astype(jnp.float32), w_update.astype(jnp.float32))
    return target_feat + jax.nn.silu(update)

def layer_one(flat_pos, flat_feat, flat_real, tables, w_send, w_radial, w_update):

    def one_block(entry):
        source_idx, target_idx, slot_live, slot_self = entry
        kernel = pair_kernel(flat_pos[target_idx], flat_real[target_idx], jnp.take(flat_pos, source_idx, axis=0), jnp.take(flat_real, source_idx, axis=0), slot_live, slot_self, w_radial.shape[1])
        message = block_message(kernel, jnp.take(flat_feat, source_idx, axis=0), w_send[0], w_radial[0])
        return block_update(flat_feat[target_idx], message, w_update[0])
    layer_out = lax.map(jax.checkpoint(one_block), tables)
    return lax.optimization_barrier(layer_out.astype(jnp.bfloat16)).astype(jnp.float32)

def layer_two_energy(flat_pos, flat_feat, flat_real, tables, w_send, w_radial, w_update, w_out, w_energy):

    def one_block(entry):
        source_idx, target_idx, slot_live, slot_self = entry
        target_real = flat_real[target_idx]
        kernel = pair_kernel(flat_pos[target_idx], target_real, jnp.take(flat_pos, source_idx, axis=0), jnp.take(flat_real, source_idx, axis=0), slot_live, slot_self, w_radial.shape[1])
        message = block_message(kernel, jnp.take(flat_feat, source_idx, axis=0), w_send[1], w_radial[1])
        second = block_update(flat_feat[target_idx], message, w_update[1])
        hidden = jnp.einsum('ci,cd->di', second.astype(jnp.bfloat16).astype(jnp.float32), w_out.astype(jnp.float32))
        per_atom = lax.optimization_barrier(jnp.sum(jax.nn.silu(hidden) * w_energy[:, None], axis=0)) * target_real
        return jnp.sum(per_atom)
    return jnp.sum(lax.map(jax.checkpoint(one_block), tables))

def reference(positions, velocities, species, neighbour_blocks, embedding, w_send, w_radial, w_update, w_out, w_energy, masses):
    grid_x, grid_y, grid_z = (positions.shape[0], positions.shape[1], positions.shape[2])
    atom_count = positions.shape[-1]
    channels = w_send.shape[-1]
    species_ext = jnp.pad(species, ((1, 1), (1, 1), (1, 1), (0, 0)))
    flat_feat = feature_table(species_ext, embedding).reshape(-1, channels, atom_count)
    flat_real = (species_ext > 0).astype(jnp.float32).reshape(-1, atom_count)
    tables = slot_tables(neighbour_blocks)
    inverse = inverse_mass(species, masses)
    padding = ((1, 1), (1, 1), (1, 1), (0, 0), (0, 0))

    def total_energy(coords):
        flat_pos = jnp.pad(coords, padding).reshape(-1, 3, atom_count)
        layer_out = layer_one(flat_pos, flat_feat, flat_real, tables, w_send, w_radial, w_update)
        grid_feat = layer_out.reshape(grid_x, grid_y, grid_z, channels, atom_count)
        flat_hidden = jnp.pad(grid_feat, padding).reshape(-1, channels, atom_count)
        return layer_two_energy(flat_pos, flat_hidden, flat_real, tables, w_send, w_radial, w_update, w_out, w_energy)

    def forces(coords):
        return -jax.grad(total_energy)(coords)
    coords = positions
    velocity = velocities
    travelled = jnp.zeros_like(positions)
    force_now = forces(coords)
    for stepno in range(STEPS):
        half_kick = velocity + 0.5 * time_step * force_now * inverse
        coords = coords + time_step * half_kick
        travelled = travelled + time_step * half_kick
        force_now = forces(coords)
        velocity = half_kick + 0.5 * time_step * force_now * inverse
    real_here = (species > 0).astype(jnp.float32)[..., None, :]
    kinetic = jnp.sum(real_here * 0.5 / inverse * velocity * velocity)
    slot_total = positions.size // 3
    factor = jnp.sqrt(target_slot * slot_total / (kinetic + tiny_eps))
    return (travelled, velocity * factor)
```

```python
import functools
import math

import jax
import jax.numpy as jnp
from jax import lax
from jax.experimental import pallas as pl
from jax.experimental.pallas import tpu as pltpu
from jax.sharding import PartitionSpec as P

soft_sq = 0.25
cut_sq = 25.0
gamma_width = 2.56
time_step = 1.0
target_slot = 0.25
tiny_eps = 1e-06
LOG2E = math.log2(math.e)
CHUNK = 32
bf16 = jnp.bfloat16
f32 = jnp.float32

SIDES = (("gx", 0), ("gy", 1), ("gz", 2))


def padded(cells):
    for axis, dim in SIDES:
        count = lax.axis_size(axis)
        ends = count - 1
        head = lax.slice_in_dim(cells, 0, 1, axis=dim)
        tail = lax.slice_in_dim(cells, cells.shape[dim] - 1, cells.shape[dim], axis=dim)
        cells = jnp.concatenate(
            [
                lax.ppermute(tail, axis, [(i, i + 1) for i in range(ends)]),
                cells,
                lax.ppermute(head, axis, [(i + 1, i) for i in range(ends)]),
            ],
            axis=dim,
        )
    return cells


def folded(grid):
    for axis, dim in reversed(SIDES):
        count = lax.axis_size(axis)
        ends = count - 1
        size = grid.shape[dim]
        low = lax.slice_in_dim(grid, 0, 1, axis=dim)
        high = lax.slice_in_dim(grid, size - 1, size, axis=dim)
        from_low = lax.ppermute(high, axis, [(i, i + 1) for i in range(ends)])
        from_high = lax.ppermute(low, axis, [(i + 1, i) for i in range(ends)])
        inner = lax.slice_in_dim(grid, 1, size - 1, axis=dim)
        first = lax.slice_in_dim(inner, 0, 1, axis=dim) + from_low
        last = lax.slice_in_dim(inner, size - 3, size - 2, axis=dim)
        if size == 3:
            grid = first + from_high
        else:
            middle = lax.slice_in_dim(inner, 1, size - 3, axis=dim)
            grid = jnp.concatenate([first, middle, last + from_high], axis=dim)
    return grid


def slot_tables(neighbour_blocks):
    size_x, size_y, size_z, slot_count = neighbour_blocks.shape
    is_live = neighbour_blocks < 27
    offset = jnp.where(is_live, neighbour_blocks, 13)
    index_x = lax.broadcasted_iota(jnp.int32, neighbour_blocks.shape, 0)
    index_y = lax.broadcasted_iota(jnp.int32, neighbour_blocks.shape, 1)
    index_z = lax.broadcasted_iota(jnp.int32, neighbour_blocks.shape, 2)
    source = (
        (index_x + offset // 9) * (size_y + 2) + (index_y + offset // 3 % 3)
    ) * (size_z + 2) + (index_z + offset % 3)
    live = jnp.sum(is_live.astype(jnp.int32), axis=-1)
    return source.reshape(-1, slot_count), live.reshape(-1)


def basis_constants(basis_count):
    step = 5.0 / basis_count
    mid = basis_count // 2
    centers = [(k + 0.5) * step for k in range(basis_count)]
    scales = [math.exp(-gamma_width * (centers[k] - centers[mid]) ** 2) for k in range(basis_count)]
    return step, mid, centers, scales


def geometry(own, cols, row0, is_self, basis_count):
    step, mid, centers, _ = basis_constants(basis_count)
    rows = slice(row0, row0 + CHUNK)
    dx = cols[rows, 0:1] - own[0:1, :]
    dy = cols[rows, 1:2] - own[1:2, :]
    dz = cols[rows, 2:3] - own[2:3, :]
    squared = jnp.minimum(dx * dx + dy * dy + dz * dz, cut_sq)
    shape = squared.shape
    j_index = lax.broadcasted_iota(jnp.int32, shape, 0) + row0
    i_index = lax.broadcasted_iota(jnp.int32, shape, 1)
    cut = (cut_sq - squared) * (1.0 / cut_sq)
    cut = jnp.where((j_index == i_index) & is_self, 0.0, cut)
    soft = squared + soft_sq
    inv = lax.rsqrt(soft)
    shift = soft * inv - centers[mid]
    bell = jnp.exp2((-gamma_width * LOG2E) * (shift * shift))
    slope = shift * (2.0 * gamma_width * step * LOG2E)
    return cut, inv, bell, jnp.exp2(slope), jnp.exp2(-slope)


def radial_powers(start, up, down, basis_count):
    mid = basis_count // 2
    powers = [None] * basis_count
    powers[mid] = start
    for k in range(mid + 1, basis_count):
        powers[k] = powers[k - 1] * up
    for k in range(mid - 1, -1, -1):
        powers[k] = powers[k + 1] * down
    return powers


def fill_kernel(store, own, cols, is_self, basis_count):
    atoms = own.shape[-1]
    for row0 in range(0, atoms, CHUNK):
        cut, _, bell, up, down = geometry(own, cols, row0, is_self, basis_count)
        for k, value in enumerate(radial_powers(cut * cut * bell, up, down, basis_count)):
            store[k, row0 : row0 + CHUNK, :] = value.astype(bf16)


def pick(species_row, table, first):
    out = None
    for s in range(first, table.shape[0]):
        hit = species_row == float(s)
        out = jnp.where(hit, table[s], 0.0 if out is None else out)
    return out


def widened(radial, value):
    return jnp.concatenate(
        [(radial[k] * value).astype(bf16) for k in range(radial.shape[0])], axis=1
    )


def silu_grad(value):
    gate = jax.nn.sigmoid(value)
    return gate * (1.0 + value * (1.0 - gate))


def dot(a, b):
    return jnp.dot(a, b, preferred_element_type=f32)


def first_kernel(target_of, src, live, pos, send_tab, feat_tab, radial, update_t, send_t,
                 h1_out, u1_out, s2_out, store):
    basis_count = radial.shape[0]
    channels, atoms = send_tab.shape[1:]
    for b, home in enumerate(target_of):
        own = pos[home]

        def slot(q, total):
            block = pos[src[b, q]]
            fill_kernel(store, own, block.T, q == 0, basis_count)
            wide = widened(radial, pick(block[3:4, :], send_tab, 1))
            return total + dot(wide, store[...].reshape(basis_count * atoms, atoms))

        total = lax.fori_loop(0, live[b], slot, jnp.zeros((channels, atoms), f32))
        update = dot(update_t[...], total.astype(bf16))
        species = own[3:4, :]
        hidden = (pick(species, feat_tab, 0) + update * jax.nn.sigmoid(update)).astype(bf16)
        h1_out[b] = hidden
        u1_out[b] = update
        s2_out[b] = jnp.where(species > 0.0, dot(send_t[...], hidden), 0.0).astype(bf16)


def second_kernel(target_of, src, live, pos, s2, h1, radial, update, update_t, out, out_t, energy,
                  g2_out, dh2_out, ds_out, store, acc):
    basis_count = radial.shape[0]
    channels, atoms = s2.shape[1:]
    acc[...] = jnp.zeros_like(acc)
    for b, home in enumerate(target_of):
        own = pos[home]

        def gather(q, total):
            where = src[b, q]
            fill_kernel(store.at[q], own, pos[where].T, q == 0, basis_count)
            wide = widened(radial, s2[where].astype(f32))
            return total + dot(wide, store[q].reshape(basis_count * atoms, atoms))

        total = lax.fori_loop(0, live[b], gather, jnp.zeros((channels, atoms), f32))
        up = dot(update_t[...], total.astype(bf16))
        second = h1[b].astype(f32) + up * jax.nn.sigmoid(up)
        hidden = dot(out_t[...], second.astype(bf16))
        real = own[3:4, :] > 0.0
        d_hidden = jnp.where(real, energy[...] * silu_grad(hidden), 0.0)
        d_second = dot(out[...], d_hidden.astype(bf16))
        dh2_out[b] = d_second
        g2 = dot(update[...], (d_second * silu_grad(up)).astype(bf16)).astype(bf16)
        g2_out[b] = g2
        wide = widened(radial, g2.astype(f32))

        def scatter(q, carry):
            flat = jnp.concatenate([store[q, k] for k in range(basis_count)], axis=1)
            where = src[b, q]
            acc[where] += lax.dot_general(
                wide, flat, (((1,), (1,)), ((), ())), preferred_element_type=f32
            )
            return carry

        lax.fori_loop(0, live[b], scatter, 0)
    ds_out[...] = acc[...].astype(bf16)


def split_rows(rel):
    row = lax.broadcasted_iota(jnp.int32, rel.shape, 0)
    rel = jnp.where(row < 3, rel, jnp.where(row == 3, 1.0, 0.0))
    high = rel.astype(bf16)
    low = (rel - high.astype(f32)).astype(bf16)
    return rel, jnp.concatenate([high, low], axis=0)


def third_kernel(target_of, src, live, pos, s2, g2, dh2, ds, u1, send_tab, radial_one, radial_two,
                 send, update, grad_out, wide, parts):
    basis_count = radial_one.shape[0]
    atoms = pos.shape[-1]
    _, _, centers, _ = basis_constants(basis_count)
    grad_out[...] = jnp.zeros_like(grad_out)
    for b, home in enumerate(target_of):
        own = pos[home]
        real = own[3:4, :] > 0.0
        dh1 = dh2[b] + dot(send[...], ds[b])
        du1 = dh1 * silu_grad(u1[b])
        g1 = jnp.where(real, dot(update[...], du1.astype(bf16)), 0.0).astype(bf16)
        wide[...] = jnp.concatenate(
            [widened(radial_one, g1.astype(f32)), widened(radial_two, g2[b].astype(f32))], axis=0
        )
        origin = own[:, 0:1]
        own_rel, own_split = split_rows(own - origin)

        def slot(q, total):
            where = src[b, q]
            block = pos[where]
            cols = block.T
            sender = jnp.concatenate(
                [pick(block[3:4, :], send_tab, 1), s2[where].astype(f32)], axis=0
            )
            parts[...] = dot(sender.T.astype(bf16), wide[...])
            pieces = []
            for row0 in range(0, atoms, CHUNK):
                cut, inv, bell, up, down = geometry(own, cols, row0, q == 0, basis_count)
                plain = jnp.zeros_like(cut)
                moment = jnp.zeros_like(cut)
                for k, value in enumerate(radial_powers(bell, up, down, basis_count)):
                    term = value * parts[row0 : row0 + CHUNK, k * atoms : (k + 1) * atoms]
                    plain = plain + term
                    moment = moment + centers[k] * term
                scaled = gamma_width * cut
                pieces.append(
                    (cut * (moment * (scaled * inv) - plain * (scaled + 2.0 / cut_sq))).astype(bf16)
                )
            slope = jnp.concatenate(pieces, axis=0)
            block_rel, block_split = split_rows(block - origin)
            at_target = dot(block_split, slope)
            at_source = lax.dot_general(
                own_split, slope, (((1,), (1,)), ((), ())), preferred_element_type=f32
            )
            at_target = at_target[:8] + at_target[8:]
            at_source = at_source[:8] + at_source[8:]
            grad_out[where] += 2.0 * (block_rel * at_source[3:4, :] - at_source)
            return total + 2.0 * (own_rel * at_target[3:4, :] - at_target)

        total = lax.fori_loop(0, live[b], slot, jnp.zeros_like(own))
        grad_out[home] += total


def call(kernel, outs, scratch, smem, args):
    return pl.pallas_call(
        kernel,
        out_shape=outs,
        in_specs=[pl.BlockSpec(memory_space=pltpu.SMEM)] * len(smem)
        + [pl.BlockSpec(memory_space=pltpu.VMEM)] * len(args),
        out_specs=[pl.BlockSpec(memory_space=pltpu.VMEM)] * len(outs),
        scratch_shapes=scratch,
        compiler_params=pltpu.CompilerParams(vmem_limit_bytes=48 << 20),
    )(*smem, *args)


def local(
    positions,
    velocities,
    species,
    neighbour_blocks,
    embedding,
    w_send,
    w_radial,
    w_update,
    w_out,
    w_energy,
    masses,
):
    grid_x, grid_y, grid_z = positions.shape[:3]
    atoms = positions.shape[-1]
    channels = w_send.shape[-1]
    basis_count = w_radial.shape[1]
    kinds = masses.shape[0]
    blocks = grid_x * grid_y * grid_z
    ext_shape = (grid_x + 2, grid_y + 2, grid_z + 2)
    ext_count = ext_shape[0] * ext_shape[1] * ext_shape[2]
    target_of = [
        ((x + 1) * ext_shape[1] + y + 1) * ext_shape[2] + z + 1
        for x in range(grid_x)
        for y in range(grid_y)
        for z in range(grid_z)
    ]
    src, live = slot_tables(neighbour_blocks)
    smem = (src, live)
    scales = jnp.array(basis_constants(basis_count)[3], f32)
    radial = jnp.broadcast_to(
        (w_radial * scales[None, :, None])[..., None], (2, basis_count, channels, atoms)
    )
    send_rows = jnp.dot(embedding, w_send[0], preferred_element_type=f32).astype(bf16).astype(f32)
    send_tab = jnp.broadcast_to(send_rows[..., None], (kinds, channels, atoms))
    feat_tab = jnp.broadcast_to(embedding.astype(f32)[..., None], (kinds, channels, atoms))
    energy = jnp.broadcast_to(w_energy[:, None], (channels, atoms))
    update_t = jnp.swapaxes(w_update, 1, 2)
    species_row = species.astype(f32)[..., None, :]
    filler = jnp.zeros((grid_x, grid_y, grid_z, 4, atoms), f32)

    def shaped(count, dtype):
        return jax.ShapeDtypeStruct((count, channels, atoms), dtype)

    def grid_of(value):
        return value.reshape((grid_x, grid_y, grid_z) + value.shape[1:])

    def flat(value):
        return value.reshape((-1,) + value.shape[3:])

    def forces(coords):
        pos = flat(padded(jnp.concatenate([coords, species_row, filler], axis=3)))
        h1, u1, s2_own = call(
            functools.partial(first_kernel, target_of),
            [shaped(blocks, bf16), shaped(blocks, f32), shaped(blocks, bf16)],
            [pltpu.VMEM((basis_count, atoms, atoms), bf16)],
            smem,
            (pos, send_tab, feat_tab, radial[0], update_t[0], w_send[1].T),
        )
        s2 = flat(padded(grid_of(s2_own)))
        g2, dh2, ds = call(
            functools.partial(second_kernel, target_of),
            [shaped(blocks, bf16), shaped(blocks, f32), shaped(ext_count, bf16)],
            [
                pltpu.VMEM((src.shape[1], basis_count, atoms, atoms), bf16),
                pltpu.VMEM((ext_count, channels, atoms), f32),
            ],
            smem,
            (pos, s2, h1, radial[1], w_update[1], update_t[1], w_out, w_out.T, energy),
        )
        ds_own = flat(folded(ds.reshape(ext_shape + ds.shape[1:])))
        (grad,) = call(
            functools.partial(third_kernel, target_of),
            [jax.ShapeDtypeStruct((ext_count, 8, atoms), f32)],
            [
                pltpu.VMEM((2 * channels, basis_count * atoms), bf16),
                pltpu.VMEM((atoms, basis_count * atoms), f32),
            ],
            smem,
            (pos, s2, g2, dh2, ds_own, u1, send_tab, radial[0], radial[1], w_send[1], w_update[0]),
        )
        total = folded(grad.reshape(ext_shape + grad.shape[1:]))
        return -total[..., :3, :]

    mass = jnp.zeros(species.shape, f32)
    for s in range(kinds):
        mass = jnp.where(species == s, masses[s], mass)
    mass = mass[..., None, :]
    inverse = 1.0 / mass
    force_now = forces(positions)
    half_kick = velocities + 0.5 * time_step * force_now * inverse
    travelled = time_step * half_kick
    coords = positions + travelled
    force_now = forces(coords)
    velocity = half_kick + 0.5 * time_step * force_now * inverse
    real_here = (species > 0).astype(f32)[..., None, :]
    local_kinetic = jnp.sum(real_here * 0.5 * mass * velocity * velocity)
    kinetic = lax.psum(local_kinetic, ("gx", "gy", "gz"))
    slot_total = (
        positions.size // 3 * lax.axis_size("gx") * lax.axis_size("gy") * lax.axis_size("gz")
    )
    factor = jnp.sqrt(target_slot * slot_total / (kinetic + tiny_eps))
    return (travelled, velocity * factor)


def solution(mesh):
    placed = (
        P("gx", "gy", "gz", None, None),
        P("gx", "gy", "gz", None, None),
        P("gx", "gy", "gz", None),
        P("gx", "gy", "gz", None),
        P(),
        P(),
        P(),
        P(),
        P(),
        P(),
        P(),
    )
    return jax.shard_map(
        local,
        mesh=mesh,
        in_specs=placed,
        out_specs=(P("gx", "gy", "gz", None, None), P("gx", "gy", "gz", None, None)),
        check_vma=False,
    )
```

```python
import functools
import math

import jax
import jax.numpy as jnp
from jax import lax
from jax.experimental import pallas as pl
from jax.experimental.pallas import tpu as pltpu
from jax.sharding import PartitionSpec as P

soft_sq = 0.25
cut_sq = 25.0
gamma_width = 2.56
time_step = 1.0
target_slot = 0.25
tiny_eps = 1e-06
LOG2E = math.log2(math.e)
CHUNK = 32
bf16 = jnp.bfloat16
f32 = jnp.float32

SIDES = (("gx", 0), ("gy", 1), ("gz", 2))


MESH = pl.DeviceIdType.MESH


def greet():
    barrier = pltpu.get_barrier_semaphore()
    places = []
    expected = 0
    for axis, _ in SIDES:
        here = lax.axis_index(axis)
        has_low, has_high = here > 0, here < lax.axis_size(axis) - 1
        for there, present in ((here - 1, has_low), (here + 1, has_high)):

            @pl.when(present)
            def _(there=there, axis=axis):
                pl.semaphore_signal(barrier, inc=1, device_id={axis: there}, device_id_type=MESH)

        expected = expected + has_low.astype(jnp.int32) + has_high.astype(jnp.int32)
        places.append((here, has_low, has_high))
    pl.semaphore_wait(barrier, expected)
    return places


def swap(stage, place, low_pair, high_pair, send_sem, recv_sem):
    axis = SIDES[stage][0]
    here, has_low, has_high = place
    sides = []
    for way, (pair, there, present) in enumerate(
        ((low_pair, here - 1, has_low), (high_pair, here + 1, has_high))
    ):
        copy = pltpu.make_async_remote_copy(
            src_ref=pair[0],
            dst_ref=pair[1],
            send_sem=send_sem.at[stage, way],
            recv_sem=recv_sem.at[stage, way],
            device_id={axis: there},
            device_id_type=MESH,
        )
        pl.when(present)(copy.start)
        sides.append((copy, present))

    def finish():
        (to_low, has_low), (to_high, has_high) = sides
        pl.when(has_low)(to_low.wait_send)
        pl.when(has_high)(to_high.wait_send)
        pl.when(has_high)(to_low.wait_recv)
        pl.when(has_low)(to_high.wait_recv)

    return finish


def spans(sizes, dim, where, full):
    index = []
    for d, size in enumerate(sizes):
        if d == dim:
            index.append(pl.ds(where, 1))
        elif d in full:
            index.append(pl.ds(0, size + 2))
        else:
            index.append(pl.ds(1, size))
    return tuple(index)


def halo_kernel(own, ext, send_sem, recv_sem, copy_sem):
    sizes = own.shape[:3]
    inner = ext.at[tuple(pl.ds(1, size) for size in sizes)]
    fill = pltpu.make_async_copy(own, inner, copy_sem)
    fill.start()
    for dim, (axis, _) in enumerate(SIDES):
        here = lax.axis_index(axis)
        for where, missing in (
            (0, here == 0),
            (sizes[dim] + 1, here == lax.axis_size(axis) - 1),
        ):

            @pl.when(missing)
            def _(dim=dim, where=where):
                index = spans(sizes, dim, where, range(dim))
                shape = tuple(part.size for part in index) + ext.shape[3:]
                ext[index] = jnp.zeros(shape, ext.dtype)

    places = greet()
    for dim in range(3):
        size = sizes[dim]

        def slab(where, full=range(dim), dim=dim):
            return ext.at[spans(sizes, dim, where, full)]

        if dim == 0:
            low, high = own.at[pl.ds(0, 1)], own.at[pl.ds(size - 1, 1)]
        else:
            low, high = slab(1), slab(size)
        finish = swap(
            dim, places[dim], (low, slab(size + 1)), (high, slab(0)), send_sem, recv_sem
        )
        if dim == 0:
            fill.wait()
        finish()


def fold_kernel(ext, own, *refs):
    lands, sums = refs[:6], (ext,) + refs[6:8]
    send_sem, recv_sem = refs[8:]
    for stage in range(3):
        dim = 2 - stage
        axis = SIDES[dim][0]
        here = lax.axis_index(axis)
        for land, missing in (
            (lands[2 * dim], here == 0),
            (lands[2 * dim + 1], here == lax.axis_size(axis) - 1),
        ):

            @pl.when(missing)
            def _(land=land):
                land[...] = jnp.zeros_like(land)

    places = greet()

    def edge(source, dim, where):
        return source.at[tuple(pl.ds(where, 1) if d == dim else slice(None) for d in range(3))]

    def send(dim, source):
        last = source.shape[dim] - 1
        return swap(
            dim,
            places[dim],
            (edge(source, dim, 0), lands[2 * dim + 1]),
            (edge(source, dim, last), lands[2 * dim]),
            send_sem,
            recv_sem,
        )

    def total(source, dim, index):
        size = source.shape[dim] - 2
        place = index[dim]
        moved = index[:dim] + (place + 1,) + index[dim + 1 :]
        flat = index[:dim] + (0,) + index[dim + 1 :]
        value = source[moved].astype(f32)
        if place == 0:
            value = value + lands[2 * dim][flat].astype(f32)
        if place == size - 1:
            value = value + lands[2 * dim + 1][flat].astype(f32)
        return value.astype(own.dtype)

    finish = send(2, ext)
    for dim in (2, 1, 0):
        source = sums[2 - dim]
        finish()
        target = own if dim == 0 else sums[3 - dim]
        shape = target.shape[:3]
        places_all = [
            (x, y, z) for x in range(shape[0]) for y in range(shape[1]) for z in range(shape[2])
        ]
        rim = [i for i in places_all if dim > 0 and i[dim - 1] in (0, shape[dim - 1] - 1)]
        for index in rim:
            target[index] = total(source, dim, index)
        if dim > 0:
            finish = send(dim - 1, target)
        for index in places_all:
            if index not in rim:
                target[index] = total(source, dim, index)


def vmem_specs(count):
    return [pl.BlockSpec(memory_space=pltpu.VMEM)] * count


def remote(collective_id):
    return pltpu.CompilerParams(
        collective_id=collective_id, has_side_effects=True, vmem_limit_bytes=48 << 20
    )


def padded(cells, collective_id):
    shape = tuple(size + 2 for size in cells.shape[:3]) + cells.shape[3:]
    return pl.pallas_call(
        halo_kernel,
        out_shape=jax.ShapeDtypeStruct(shape, cells.dtype),
        in_specs=vmem_specs(1),
        out_specs=vmem_specs(1)[0],
        scratch_shapes=[
            pltpu.SemaphoreType.DMA((3, 2)),
            pltpu.SemaphoreType.DMA((3, 2)),
            pltpu.SemaphoreType.DMA,
        ],
        compiler_params=remote(collective_id),
    )(cells)


def folded(grid, collective_id):
    x, y, z = (size - 2 for size in grid.shape[:3])
    tail = grid.shape[3:]
    landings = [(1, y, z), (1, y, z), (x + 2, 1, z), (x + 2, 1, z), (x + 2, y + 2, 1), (x + 2, y + 2, 1)]
    sums = [(x + 2, y + 2, z), (x + 2, y, z)]
    return pl.pallas_call(
        fold_kernel,
        out_shape=jax.ShapeDtypeStruct((x, y, z) + tail, grid.dtype),
        in_specs=vmem_specs(1),
        out_specs=vmem_specs(1)[0],
        scratch_shapes=[pltpu.VMEM(shape + tail, grid.dtype) for shape in landings + sums]
        + [pltpu.SemaphoreType.DMA((3, 2)), pltpu.SemaphoreType.DMA((3, 2))],
        compiler_params=remote(collective_id),
    )(grid)


def thermostat_kernel(slot_total, part, velocity, out, *refs):
    inbox, sums, (send_sem, recv_sem) = refs[:3], refs[3:6], refs[6:]
    barrier = pltpu.get_barrier_semaphore()
    peers = 0
    for axis, _ in SIDES:
        count = lax.axis_size(axis)
        for t in range(1, count):
            there = lax.rem(lax.axis_index(axis) + t, count)
            pl.semaphore_signal(barrier, inc=1, device_id={axis: there}, device_id_type=MESH)
            peers += 1
    pl.semaphore_wait(barrier, peers)
    current = part
    base = 0
    for stage, (axis, _) in enumerate(SIDES):
        count = lax.axis_size(axis)
        copies = []
        for t in range(1, count):
            there = lax.rem(lax.axis_index(axis) + t, count)
            copy = pltpu.make_async_remote_copy(
                src_ref=current,
                dst_ref=inbox[stage].at[t - 1],
                send_sem=send_sem.at[base],
                recv_sem=recv_sem.at[base],
                device_id={axis: there},
                device_id_type=MESH,
            )
            copy.start()
            copies.append(copy)
            base += 1
        value = current[...]
        for t, copy in enumerate(copies):
            copy.wait()
            value = value + inbox[stage][t]
        sums[stage][...] = value
        current = sums[stage]
    kinetic = jnp.sum(value, keepdims=True)
    factor = jnp.sqrt(target_slot * slot_total / (kinetic + tiny_eps))
    for x in range(velocity.shape[0]):
        for y in range(velocity.shape[1]):
            for z in range(velocity.shape[2]):
                out[x, y, z] = velocity[x, y, z] * factor


def thermostat(part, velocity, slot_total, collective_id):
    counts = [lax.axis_size(axis) for axis, _ in SIDES]
    peers = sum(count - 1 for count in counts)
    return pl.pallas_call(
        functools.partial(thermostat_kernel, float(slot_total)),
        out_shape=jax.ShapeDtypeStruct(velocity.shape, velocity.dtype),
        in_specs=vmem_specs(2),
        out_specs=vmem_specs(1)[0],
        scratch_shapes=[pltpu.VMEM((max(count - 1, 1),) + part.shape, f32) for count in counts]
        + [pltpu.VMEM(part.shape, f32)] * 3
        + [pltpu.SemaphoreType.DMA((peers,)), pltpu.SemaphoreType.DMA((peers,))],
        compiler_params=remote(collective_id),
    )(part, velocity)


def slot_tables(neighbour_blocks):
    size_x, size_y, size_z, slot_count = neighbour_blocks.shape
    is_live = neighbour_blocks < 27
    offset = jnp.where(is_live, neighbour_blocks, 13)
    index_x = lax.broadcasted_iota(jnp.int32, neighbour_blocks.shape, 0)
    index_y = lax.broadcasted_iota(jnp.int32, neighbour_blocks.shape, 1)
    index_z = lax.broadcasted_iota(jnp.int32, neighbour_blocks.shape, 2)
    source = (
        (index_x + offset // 9) * (size_y + 2) + (index_y + offset // 3 % 3)
    ) * (size_z + 2) + (index_z + offset % 3)
    live = jnp.sum(is_live.astype(jnp.int32), axis=-1)
    return source.reshape(-1, slot_count), live.reshape(-1)


def basis_constants(basis_count):
    step = 5.0 / basis_count
    mid = basis_count // 2
    centers = [(k + 0.5) * step for k in range(basis_count)]
    scales = [math.exp(-gamma_width * (centers[k] - centers[mid]) ** 2) for k in range(basis_count)]
    return step, mid, centers, scales


def geometry(own, cols, row0, is_self, basis_count):
    step, mid, centers, _ = basis_constants(basis_count)
    rows = slice(row0, row0 + CHUNK)
    dx = cols[rows, 0:1] - own[0:1, :]
    dy = cols[rows, 1:2] - own[1:2, :]
    dz = cols[rows, 2:3] - own[2:3, :]
    squared = jnp.minimum(dx * dx + dy * dy + dz * dz, cut_sq)
    shape = squared.shape
    j_index = lax.broadcasted_iota(jnp.int32, shape, 0) + row0
    i_index = lax.broadcasted_iota(jnp.int32, shape, 1)
    cut = (cut_sq - squared) * (1.0 / cut_sq)
    cut = jnp.where((j_index == i_index) & is_self, 0.0, cut)
    soft = squared + soft_sq
    inv = lax.rsqrt(soft)
    shift = soft * inv - centers[mid]
    bell = jnp.exp2((-gamma_width * LOG2E) * (shift * shift))
    slope = shift * (2.0 * gamma_width * step * LOG2E)
    return cut, inv, bell, jnp.exp2(slope), jnp.exp2(-slope)


def radial_powers(start, up, down, basis_count):
    mid = basis_count // 2
    powers = [None] * basis_count
    powers[mid] = start
    for k in range(mid + 1, basis_count):
        powers[k] = powers[k - 1] * up
    for k in range(mid - 1, -1, -1):
        powers[k] = powers[k + 1] * down
    scales = basis_constants(basis_count)[3]
    return [power * scale if scale != 1.0 else power for power, scale in zip(powers, scales)]


def fill_kernel(store, own, cols, is_self, basis_count):
    atoms = own.shape[-1]
    for row0 in range(0, atoms, CHUNK):
        cut, _, bell, up, down = geometry(own, cols, row0, is_self, basis_count)
        for k, value in enumerate(radial_powers(cut * cut * bell, up, down, basis_count)):
            store[row0 : row0 + CHUNK, k * atoms : (k + 1) * atoms] = value.astype(bf16)


def pick(species_row, table, first):
    out = None
    for s in range(first, table.shape[0]):
        hit = species_row == float(s)
        out = jnp.where(hit, table[s], 0.0 if out is None else out)
    return out


def split(value):
    high = value.astype(bf16)
    return high, (value - high.astype(f32)).astype(bf16)


def dot_split(a, value):
    high, low = split(value)
    return dot(a, high) + dot(a, low)


def widened_split(radial, value):
    pairs = [split(radial[k] * value) for k in range(radial.shape[0])]
    return [jnp.concatenate(part, axis=1) for part in zip(*pairs)]


def held(value):
    return value.astype(bf16).astype(f32)


def narrowed(radial, sums):
    atoms = radial.shape[-1]
    return sum(
        radial[k] * sums[:, k * atoms : (k + 1) * atoms] for k in range(radial.shape[0])
    )


def silu_grad(value):
    gate = jax.nn.sigmoid(value)
    return gate * (1.0 + value * (1.0 - gate))


def dot(a, b):
    return jnp.dot(a, b, preferred_element_type=f32)


def first_kernel(target_of, src, live, pos, send_tab, feat_tab, radial, update_t, send_t,
                 h1_out, u1_out, s2_out, store, sums):
    basis_count = radial.shape[0]
    channels, atoms = send_tab.shape[1:]
    for b, home in enumerate(target_of):
        own = pos[home]

        sums[...] = jnp.zeros_like(sums)

        def slot(q, carry):
            block = pos[src[b, q]]
            fill_kernel(store, own, block.T, q == 0, basis_count)
            sums[...] += dot(pick(block[3:4, :], send_tab, 1).astype(bf16), store[...])
            return carry

        lax.fori_loop(0, live[b], slot, 0)
        total = narrowed(radial, sums)
        update = dot(update_t[...], total.astype(bf16))
        species = own[3:4, :]
        hidden = (pick(species, feat_tab, 0) + update * jax.nn.sigmoid(update)).astype(bf16)
        h1_out[b] = hidden
        u1_out[b] = update
        s2_out[b] = jnp.where(species > 0.0, dot(send_t[...], hidden), 0.0).astype(bf16)


def second_kernel(target_of, src, live, pos, s2, h1, radial, update, update_t, out, out_t, energy,
                  g2_out, dh2_out, ds_out, store, acc, sums):
    basis_count = radial.shape[0]
    channels, atoms = s2.shape[1:]
    acc[...] = jnp.zeros_like(acc)
    for b, home in enumerate(target_of):
        own = pos[home]

        sums[...] = jnp.zeros_like(sums)

        def gather(q, carry):
            where = src[b, q]
            fill_kernel(store.at[q], own, pos[where].T, q == 0, basis_count)
            sums[...] += dot(s2[where], store[q])
            return carry

        lax.fori_loop(0, live[b], gather, 0)
        total = narrowed(radial, sums)
        up = dot(update_t[...], total.astype(bf16))
        second = h1[b].astype(f32) + up * jax.nn.sigmoid(up)
        hidden = dot(out_t[...], second.astype(bf16))
        real = own[3:4, :] > 0.0
        d_hidden = jnp.where(real, energy[...] * silu_grad(hidden), 0.0)
        d_second = held(dot_split(out[...], d_hidden))
        dh2_out[b] = d_second
        g2 = dot_split(update[...], d_second * silu_grad(up)).astype(bf16)
        g2_out[b] = g2
        wide = jnp.concatenate(widened_split(radial, g2.astype(f32)), axis=0)

        def scatter(q, carry):
            where = src[b, q]
            both = lax.dot_general(
                wide, store[q], (((1,), (1,)), ((), ())), preferred_element_type=f32
            )
            acc[where] += both[:channels] + both[channels:]
            return carry

        lax.fori_loop(0, live[b], scatter, 0)
    ds_out[...] = acc[...].astype(bf16)


def split_rows(rel):
    row = lax.broadcasted_iota(jnp.int32, rel.shape, 0)
    rel = jnp.where(row < 3, rel, jnp.where(row == 3, 1.0, 0.0))
    high = rel.astype(bf16)
    low = (rel - high.astype(f32)).astype(bf16)
    return rel, jnp.concatenate([high, low], axis=0)


def third_kernel(target_of, src, live, pos, s2, g2, dh2, ds, u1, send_tab, radial_one, radial_two,
                 send, update, grad_out, wide, parts):
    basis_count = radial_one.shape[0]
    atoms = pos.shape[-1]
    _, _, centers, _ = basis_constants(basis_count)
    grad_out[...] = jnp.zeros_like(grad_out)
    for b, home in enumerate(target_of):
        own = pos[home]
        real = own[3:4, :] > 0.0
        dh1 = held(dh2[b] + dot(send[...], ds[b]))
        du1 = dh1 * silu_grad(u1[b])
        g1 = jnp.where(real, dot_split(update[...], du1), 0.0).astype(bf16)
        wide[...] = jnp.concatenate(
            widened_split(radial_one, g1.astype(f32))
            + widened_split(radial_two, g2[b].astype(f32)),
            axis=0,
        )
        origin = own[:, 0:1]
        own_rel, own_split = split_rows(own - origin)

        def slot(q, total):
            where = src[b, q]
            block = pos[where]
            cols = block.T
            senders = (pick(block[3:4, :], send_tab, 1), s2[where].astype(f32))
            turned = [sender.T.astype(bf16) for sender in (senders[0], senders[1])]
            flipped = jnp.concatenate([turned[0], turned[0], turned[1], turned[1]], axis=1)
            parts[...] = dot(flipped, wide[...])
            pieces = []
            for row0 in range(0, atoms, CHUNK):
                cut, inv, bell, up, down = geometry(own, cols, row0, q == 0, basis_count)
                plain = jnp.zeros_like(cut)
                moment = jnp.zeros_like(cut)
                for k, value in enumerate(radial_powers(bell, up, down, basis_count)):
                    term = value * parts[row0 : row0 + CHUNK, k * atoms : (k + 1) * atoms]
                    plain = plain + term
                    moment = moment + centers[k] * term
                scaled = gamma_width * cut
                pieces.append(
                    (cut * (moment * (scaled * inv) - plain * (scaled + 2.0 / cut_sq)))
                )
            high, low = split(jnp.concatenate(pieces, axis=0))
            block_rel, block_split = split_rows(block - origin)
            at_target = dot(block_split, high) + dot(block_split, low)
            at_source = sum(
                lax.dot_general(
                    own_split, part, (((1,), (1,)), ((), ())), preferred_element_type=f32
                )
                for part in (high, low)
            )
            at_target = at_target[:8] + at_target[8:]
            at_source = at_source[:8] + at_source[8:]
            grad_out[where] += 2.0 * (block_rel * at_source[3:4, :] - at_source)
            return total + 2.0 * (own_rel * at_target[3:4, :] - at_target)

        total = lax.fori_loop(0, live[b], slot, jnp.zeros_like(own))
        grad_out[home] += total


def call(kernel, outs, scratch, smem, args):
    return pl.pallas_call(
        kernel,
        out_shape=outs,
        in_specs=[pl.BlockSpec(memory_space=pltpu.SMEM)] * len(smem)
        + [pl.BlockSpec(memory_space=pltpu.VMEM)] * len(args),
        out_specs=[pl.BlockSpec(memory_space=pltpu.VMEM)] * len(outs),
        scratch_shapes=scratch,
        compiler_params=pltpu.CompilerParams(vmem_limit_bytes=48 << 20),
    )(*smem, *args)


def local(
    positions,
    velocities,
    species,
    neighbour_blocks,
    embedding,
    w_send,
    w_radial,
    w_update,
    w_out,
    w_energy,
    masses,
):
    grid_x, grid_y, grid_z = positions.shape[:3]
    atoms = positions.shape[-1]
    channels = w_send.shape[-1]
    basis_count = w_radial.shape[1]
    kinds = masses.shape[0]
    blocks = grid_x * grid_y * grid_z
    ext_shape = (grid_x + 2, grid_y + 2, grid_z + 2)
    ext_count = ext_shape[0] * ext_shape[1] * ext_shape[2]
    target_of = [
        ((x + 1) * ext_shape[1] + y + 1) * ext_shape[2] + z + 1
        for x in range(grid_x)
        for y in range(grid_y)
        for z in range(grid_z)
    ]
    src, live = slot_tables(neighbour_blocks)
    smem = (src, live)
    radial = jnp.broadcast_to(
        w_radial[..., None], (2, basis_count, channels, atoms)
    )
    send_rows = jnp.dot(embedding, w_send[0], preferred_element_type=f32).astype(bf16).astype(f32)
    send_tab = jnp.broadcast_to(send_rows[..., None], (kinds, channels, atoms))
    feat_tab = jnp.broadcast_to(embedding.astype(f32)[..., None], (kinds, channels, atoms))
    energy = jnp.broadcast_to(w_energy[:, None], (channels, atoms))
    update_t = jnp.swapaxes(w_update, 1, 2)
    species_row = species.astype(f32)[..., None, :]
    filler = jnp.zeros((grid_x, grid_y, grid_z, 4, atoms), f32)

    def shaped(count, dtype):
        return jax.ShapeDtypeStruct((count, channels, atoms), dtype)

    def grid_of(value):
        return value.reshape((grid_x, grid_y, grid_z) + value.shape[1:])

    def flat(value):
        return value.reshape((-1,) + value.shape[3:])

    def forces(coords):
        pos = flat(padded(jnp.concatenate([coords, species_row, filler], axis=3), 0))
        h1, u1, s2_own = call(
            functools.partial(first_kernel, target_of),
            [shaped(blocks, bf16), shaped(blocks, f32), shaped(blocks, bf16)],
            [
                pltpu.VMEM((atoms, basis_count * atoms), bf16),
                pltpu.VMEM((channels, basis_count * atoms), f32),
            ],
            smem,
            (pos, send_tab, feat_tab, radial[0], update_t[0], w_send[1].T),
        )
        s2 = flat(padded(grid_of(s2_own), 1))
        g2, dh2, ds = call(
            functools.partial(second_kernel, target_of),
            [shaped(blocks, bf16), shaped(blocks, f32), shaped(ext_count, bf16)],
            [
                pltpu.VMEM((src.shape[1], atoms, basis_count * atoms), bf16),
                pltpu.VMEM((ext_count, channels, atoms), f32),
                pltpu.VMEM((channels, basis_count * atoms), f32),
            ],
            smem,
            (pos, s2, h1, radial[1], w_update[1], update_t[1], w_out, w_out.T, energy),
        )
        ds_own = flat(folded(ds.reshape(ext_shape + ds.shape[1:]), 2))
        (grad,) = call(
            functools.partial(third_kernel, target_of),
            [jax.ShapeDtypeStruct((ext_count, 8, atoms), f32)],
            [
                pltpu.VMEM((4 * channels, basis_count * atoms), bf16),
                pltpu.VMEM((atoms, basis_count * atoms), f32),
            ],
            smem,
            (pos, s2, g2, dh2, ds_own, u1, send_tab, radial[0], radial[1], w_send[1], w_update[0]),
        )
        total = folded(grad.reshape(ext_shape + grad.shape[1:]), 3)
        return -total[..., :3, :]

    mass = jnp.zeros(species.shape, f32)
    for s in range(kinds):
        mass = jnp.where(species == s, masses[s], mass)
    mass = mass[..., None, :]
    inverse = 1.0 / mass
    force_now = forces(positions)
    half_kick = velocities + 0.5 * time_step * force_now * inverse
    travelled = time_step * half_kick
    coords = positions + travelled
    force_now = forces(coords)
    velocity = half_kick + 0.5 * time_step * force_now * inverse
    real_here = (species > 0).astype(f32)[..., None, :]
    part = jnp.sum(real_here * 0.5 * mass * velocity * velocity, axis=(0, 1, 2, 3))
    part = jnp.broadcast_to(part * 0.125, (8, atoms))
    slot_total = (
        positions.size // 3 * lax.axis_size("gx") * lax.axis_size("gy") * lax.axis_size("gz")
    )
    return (travelled, thermostat(part, velocity, slot_total, 4))


def solution(mesh):
    placed = (
        P("gx", "gy", "gz", None, None),
        P("gx", "gy", "gz", None, None),
        P("gx", "gy", "gz", None),
        P("gx", "gy", "gz", None),
        P(),
        P(),
        P(),
        P(),
        P(),
        P(),
        P(),
    )
    return jax.shard_map(
        local,
        mesh=mesh,
        in_specs=placed,
        out_specs=(P("gx", "gy", "gz", None, None), P("gx", "gy", "gz", None, None)),
        check_vma=False,
    )
```
